32 devices in a mesh: stn: 8 (over z, core), chan: 4 (over y, x).
Axes of the slice: x: 2, y: 2, z: 4, core: 2. Of those that a mesh axis runs over, the one named last changes fastest.
Arguments:
- voltages: bfloat16 [64, 32, 2, 1024], P('stn', 'chan'), may hold values from -6 to 6
- filter_taps: float32 [16, 1024], replicated, may hold values from -1.5 to 1.5
Outputs:
- visibilities: bfloat16 [1024, 2, 64, 64], P('chan', None, 'stn')
The draws below stay inside these ranges and needn't reach their ends.
All inputs are finite; a program needn't handle non-finite values.
Results may differ from the reference program's by a relative error of at most 0.0069.
Values may be sent and summed in bfloat16 or wider, within the bound.
A program may use at most 64 MiB of HBM per device.

```python
import math
import jax
import jax.numpy as jnp
from jax import lax

NFFT = 1024
TAPS = 16
STN_DEV = 4
INPUTS = 64
SPECTRA = 32
N_CHAN = 4


def level_of(rng, dims, shards, smallest, high):
    factor_of, own = 1.0, jax.random.fold_in(rng, 6)
    for position, blocks in shards:
        steps = jnp.exp(jax.random.uniform(jax.random.fold_in(own, position), (blocks,), jnp.float32, smallest / len(shards), high / len(shards)))
        factor_of = factor_of * jnp.repeat(steps, dims[position] // blocks).reshape([-1 if axis == position else 1 for axis in range(len(dims))])
    return factor_of


def normal_values(own_key, shape, deviation, reach, split=(), kind=jnp.bfloat16):
    values = jax.random.normal(own_key, shape, jnp.float32) * deviation
    if len(split) > 0:
        values = level_of(own_key, shape, split, -0.22, 0.18) * values
    return jnp.clip(values, min=-reach, max=reach).astype(kind)


def setup_inputs(seed: int = 0) -> dict:
    splits = jax.random.split(jax.random.key(seed), 3)
    return {
        "voltages": normal_values(splits[0], (INPUTS, SPECTRA, 2, NFFT), 1.0, 6.0, ((0, 8), (1, 4))),
        "filter_taps": normal_values(splits[1], (TAPS, NFFT), TAPS ** -0.5, 1.5, (), jnp.float32),
    }


def fourier_matrix(points):
    sample_index = jnp.arange(points, dtype=jnp.int32)
    phase = sample_index[:, None] * sample_index[None, :] % points
    angle = phase.astype(jnp.float32) * (2.0 * math.pi / points)
    norm_factor = 1.0 / math.sqrt(points)
    cosine = (jnp.cos(angle) * norm_factor).astype(jnp.bfloat16)
    sine_part = (-jnp.sin(angle) * norm_factor).astype(jnp.bfloat16)
    upper_rows = jnp.stack([cosine, sine_part], axis=2)
    lower_rows = jnp.stack([-sine_part, cosine], axis=2)
    return jnp.concatenate([upper_rows, lower_rows], axis=0).reshape(2 * points, 2 * points)

def reference(voltages, filter_taps):
    inputs_all, spectra_all, parts, points = voltages.shape
    tap_count = filter_taps.shape[0]
    group_size = 2 * STN_DEV
    matrix = fourier_matrix(points).astype(jnp.float32)

    def channelise(batch_volts):
        widened = batch_volts.astype(jnp.float32)
        padded = jnp.concatenate([jnp.zeros((group_size, tap_count - 1, parts, points), jnp.float32), widened], axis=1)
        filtered = jnp.zeros(widened.shape, jnp.float32)
        for tap_index in range(tap_count):
            offset = tap_count - 1 - tap_index
            filtered = filtered + filter_taps[tap_index][None, None, None, :] * padded[:, offset:offset + spectra_all]
        rounded = lax.optimization_barrier(filtered.astype(jnp.bfloat16))
        flat = rounded.astype(jnp.float32).reshape(group_size * spectra_all, parts * points)
        transformed = jnp.dot(flat, matrix, precision=lax.Precision.HIGHEST)
        return transformed.reshape(group_size, spectra_all, points, parts).astype(jnp.bfloat16)
    grouped = voltages.reshape(inputs_all // group_size, group_size, spectra_all, parts, points)
    spectra = lax.map(channelise, grouped).reshape(inputs_all, spectra_all, points, parts)
    spectra = spectra.transpose(2, 3, 0, 1)
    block_size = points // N_CHAN
    blocks = spectra.reshape(points // block_size, block_size, parts, inputs_all, spectra_all)

    def correlate(block_data):
        widened = block_data.astype(jnp.float32)
        swapped = jnp.stack([widened[:, 1], -widened[:, 0]], axis=1)
        real_part = jnp.einsum('kcas,kcbs->kab', widened, widened, precision=lax.Precision.HIGHEST)
        imag_part = jnp.einsum('kcas,kcbs->kab', swapped, widened, precision=lax.Precision.HIGHEST)
        return (jnp.stack([real_part, imag_part], axis=1) * (1.0 / spectra_all)).astype(jnp.bfloat16)
    result = lax.map(correlate, blocks)
    return result.reshape(points, parts, inputs_all, inputs_all)
```

```python
import functools
import math

import jax
import jax.numpy as jnp
import numpy as np
from jax import lax
from jax.experimental import pallas as pl
from jax.experimental.pallas import tpu as pltpu
from jax.sharding import PartitionSpec as P

MESH = pl.DeviceIdType.MESH
NT = (((1,), (1,)), ((), ()))
LANES = 128
SUB = 8


def from_behind(array, axis, by):
    devices = lax.axis_size(axis)
    pairs = [(i, i + by) for i in range(devices) if 0 <= i + by < devices]
    return lax.ppermute(array, axis, pairs)


def passed_along(value, axis, steps):
    count = lax.axis_size(axis)
    pairs = [(source, (source + steps) % count) for source in range(count)]
    return lax.ppermute(value, axis, pairs)


def fourier_matrix(points):
    sample_index = jnp.arange(points, dtype=jnp.int32)
    phase = sample_index[:, None] * sample_index[None, :] % points
    angle = phase.astype(jnp.float32) * (2.0 * math.pi / points)
    norm_factor = 1.0 / math.sqrt(points)
    cosine = (jnp.cos(angle) * norm_factor).astype(jnp.bfloat16)
    sine_part = (-jnp.sin(angle) * norm_factor).astype(jnp.bfloat16)
    upper_rows = jnp.stack([cosine, sine_part], axis=2)
    lower_rows = jnp.stack([-sine_part, cosine], axis=2)
    return jnp.concatenate([upper_rows, lower_rows], axis=0).reshape(2 * points, 2 * points)


def history_frames(voltages, history_len):
    frames_here = voltages.shape[1]
    shift_count = (history_len - 1) // frames_here + 1
    earlier = []
    for distance in range(1, shift_count + 1):
        keep_count = min(frames_here, history_len - (distance - 1) * frames_here)
        received_frames = from_behind(voltages[:, frames_here - keep_count :], "chan", distance)
        earlier = [received_frames] + earlier
    return jnp.concatenate(earlier + [voltages], axis=1)


def correlate(local_block, swapped, other_block, factor):
    real_part = jnp.einsum(
        "kcas,kcbs->kab", local_block, other_block, preferred_element_type=jnp.float32
    )
    imag_part = jnp.einsum(
        "kcas,kcbs->kab", swapped, other_block, preferred_element_type=jnp.float32
    )
    return jnp.stack([real_part, imag_part], axis=1) * factor


def mirrored(product):
    return jnp.stack(
        [jnp.swapaxes(product[:, 0], 1, 2), -jnp.swapaxes(product[:, 1], 1, 2)], axis=1
    )


def place_block(buffer, product, chan_start, slot_index):
    columns = product.shape[3]
    anchor = jnp.int32(0)
    return lax.dynamic_update_slice(
        buffer, product, (jnp.int32(chan_start), anchor, anchor, slot_index * columns)
    )


def per_device(voltages, filter_taps):
    inputs_here, frames_here, parts, points = voltages.shape
    tap_count = filter_taps.shape[0]
    extended = history_frames(voltages, tap_count - 1)
    filtered = jnp.zeros(voltages.shape, jnp.float32)
    for tap_index in range(tap_count):
        offset = tap_count - 1 - tap_index
        filtered = filtered + filter_taps[tap_index][None, None, None, :] * extended[
            :, offset : offset + frames_here
        ].astype(jnp.float32)
    filtered = filtered.astype(jnp.bfloat16).reshape(inputs_here, frames_here, parts * points)
    matrix = fourier_matrix(points)
    spectra = jnp.einsum("isr,rq->qis", filtered, matrix, preferred_element_type=jnp.float32)
    spectra = spectra.reshape(points, parts, inputs_here, frames_here).astype(jnp.bfloat16)
    local_block = lax.all_to_all(spectra, "chan", split_axis=0, concat_axis=3, tiled=True)
    cycle_size = lax.axis_size("stn")
    position = lax.axis_index("stn")
    halfway = cycle_size // 2
    channels = local_block.shape[0]
    factor = 1.0 / local_block.shape[3]
    swapped = jnp.stack([local_block[:, 1], -local_block[:, 0]], axis=1)
    row_sums = jnp.zeros((channels, parts, inputs_here, cycle_size * inputs_here), jnp.float32)
    row_sums = place_block(
        row_sums, correlate(local_block, swapped, local_block, factor), 0, position
    )
    mirror = jnp.zeros(row_sums.shape, jnp.bfloat16)

    def cycle_turn(step_index, carry):
        moving_block, row_sums, mirror = carry
        moving_block = passed_along(moving_block, "stn", -1)
        slot_index = (position + step_index) % cycle_size
        is_kept = jnp.logical_or(step_index < halfway, position < halfway)
        product = jnp.where(is_kept, correlate(local_block, swapped, moving_block, factor), 0.0)
        row_sums = place_block(row_sums, product, 0, slot_index)
        outgoing = mirrored(product).astype(jnp.bfloat16)
        mirror = place_block(mirror, outgoing, 0, slot_index)
        return (moving_block, row_sums, mirror)

    moving_block, row_sums, mirror = lax.fori_loop(
        1, halfway + 1, cycle_turn, (local_block, row_sums, mirror)
    )
    returned = lax.all_to_all(mirror, "stn", split_axis=3, concat_axis=3, tiled=True)
    row_sums = row_sums + returned.astype(jnp.float32)
    return row_sums.astype(jnp.bfloat16)


def fourier_rows(points):
    index = np.arange(points, dtype=np.int64)
    angle = (index[:, None] * index[None, :] % points).astype(np.float64) * (2.0 * np.pi / points)
    norm_factor = 1.0 / math.sqrt(points)
    both = np.concatenate([np.cos(angle) * norm_factor, -np.sin(angle) * norm_factor], axis=1)
    return both.astype(np.float32).astype(jnp.bfloat16)


def fx_kernel(
    n_stn, n_chan, frames, points, v_ref, taps_ref, four_hbm, out_ref,
    four, xin, xf, rhs, spec, recv, rows_f, prod, gath,
    four_sem, s1, r1, s2, r2, s3, r3,
):
    devices = n_stn * n_chan
    p = lax.axis_index("stn")
    q = lax.axis_index("chan")
    me = p * n_chan + q
    group = q * n_stn + p
    chans = points // devices
    tap_count = taps_ref.shape[0]
    lane_tiles = points // LANES
    n_four = four_sem.shape[0]
    four_rows = points // n_four
    n_part = s3.shape[0]
    part_rows = chans // n_part

    def four_copy(step):
        chunk = lax.rem(group // (four_rows // chans) + step, n_four)
        rows = pl.ds(pl.multiple_of(chunk * four_rows, four_rows), four_rows)
        return chunk, pltpu.make_async_copy(four_hbm.at[rows], four.at[rows], four_sem.at[chunk])

    for step in range(n_four):
        four_copy(step)[1].start()

    barrier = pltpu.get_barrier_semaphore()

    def greet(step, carry):
        other = lax.rem(me + step, devices)
        pl.semaphore_signal(
            barrier, inc=1, device_id=(other // n_chan, lax.rem(other, n_chan)), device_id_type=MESH
        )
        return carry

    lax.fori_loop(1, devices, greet, 0)
    pl.semaphore_wait(barrier, devices - 1)

    def in_copy(to, source):
        return pltpu.make_async_remote_copy(
            src_ref=v_ref.at[to], dst_ref=xin.at[source], send_sem=s1.at[to], recv_sem=r1.at[source],
            device_id=(p, to), device_id_type=MESH,
        )

    for step in range(1, n_chan):
        in_copy(lax.rem(q + step, n_chan), q).start()

    pad = xf.shape[2] - frames
    per = frames // n_chan
    xf[:, :, :pad, :] = jnp.zeros((xf.shape[0], xf.shape[1], pad, LANES), jnp.float32)

    def widen(ref, source):
        rows = pl.ds(pl.multiple_of(pad + source * per, per), per)
        for tile in range(lane_tiles):
            xf[:, tile, rows, :] = ref[:, :, tile * LANES : (tile + 1) * LANES].astype(jnp.float32)

    widen(v_ref.at[q], q)
    for step in range(1, n_chan):
        source = lax.rem(q + step, n_chan)
        in_copy(source, source).wait_recv()
        widen(xin.at[source], source)

    def fir(e, carry):
        for c in range(2):
            for tile in range(lane_tiles):
                lanes = slice(tile * LANES, (tile + 1) * LANES)
                total = jnp.zeros((frames, LANES), jnp.float32)
                for tap in range(tap_count):
                    total = total + taps_ref[tap : tap + 1, lanes] * xf[
                        2 * e + c, tile, pad - tap : pad - tap + frames, :
                    ]
                here = pl.ds(pl.multiple_of((2 * e + c) * frames, frames), frames)
                swap = pl.ds(pl.multiple_of((2 * e + 1 - c) * frames, frames), frames)
                rhs[here, lanes] = total.astype(jnp.bfloat16)
                other = slice(points + tile * LANES, points + (tile + 1) * LANES)
                rhs[swap, other] = (total if c == 0 else -total).astype(jnp.bfloat16)
        return carry

    lax.fori_loop(0, xf.shape[0] // 2, fir, 0)

    def spec_copy(to, source):
        to_p, to_q = lax.rem(to, n_stn), to // n_stn
        rows = pl.ds(pl.multiple_of(to * chans, chans), chans)
        return pltpu.make_async_remote_copy(
            src_ref=spec.at[rows], dst_ref=recv.at[source], send_sem=s2.at[to], recv_sem=r2.at[source],
            device_id=(to_p, to_q), device_id_type=MESH,
        )

    for step in range(n_four):
        chunk, copy = four_copy(step)
        copy.wait()
        rows = pl.ds(pl.multiple_of(chunk * four_rows, four_rows), four_rows)
        spec[rows, :] = lax.dot_general(
            four[rows, :], rhs[...], NT, preferred_element_type=jnp.float32
        ).astype(jnp.bfloat16)
        for sub in range(four_rows // chans):
            to = chunk * (four_rows // chans) + sub

            @pl.when(to != group)
            def _():
                spec_copy(to, me).start()

    lane = lax.broadcasted_iota(jnp.int32, (chans, LANES), 1)
    half, quarter = LANES // 2, LANES // 4

    def spread(block, source):
        wide = block.astype(jnp.float32)
        by1, by2, by3 = (pltpu.roll(wide, quarter * n, 1) for n in (1, 2, 3))
        first = jnp.where(lane < half, wide, jnp.where(lane < half + quarter, by1, -by3))
        second = jnp.where(lane < half, by2, jnp.where(lane < half + quarter, by3, -by1))
        rows_f[pl.ds(pl.multiple_of(2 * source * chans, chans), chans), :] = first
        rows_f[pl.ds(pl.multiple_of((2 * source + 1) * chans, chans), chans), :] = second

    spread(spec[pl.ds(pl.multiple_of(group * chans, chans), chans), :], me)

    def take(step, carry):
        source = lax.rem(me + step, devices)
        spec_copy(source, source).wait_recv()
        spread(recv[source], source)
        return carry

    lax.fori_loop(1, devices, take, 0)

    def prod_copy(to, source, part):
        rows = pl.ds(part * part_rows, part_rows)
        return pltpu.make_async_remote_copy(
            src_ref=prod.at[to, rows], dst_ref=gath.at[source, rows],
            send_sem=s3.at[part, to], recv_sem=r3.at[part, source],
            device_id=(to, q), device_id_type=MESH,
        )

    inputs = rows_f.shape[0] // chans
    in_here = inputs // n_stn
    left = lax.broadcasted_iota(jnp.int32, (inputs, LANES), 1) < half
    for part in range(n_part):
        for k in range(part * part_rows, (part + 1) * part_rows):
            lhs = rows_f[pl.ds(k, inputs, stride=chans), :]
            low = jnp.where(left, lhs, 0.0)
            both = jnp.concatenate([low, pltpu.roll(low, half, 1)], axis=0).astype(jnp.bfloat16)
            result = lax.dot_general(
                lhs.astype(jnp.bfloat16), both, NT, preferred_element_type=jnp.float32
            ) * (1.0 / frames)
            prod[:, k] = result.reshape(n_stn, in_here, LANES).astype(jnp.bfloat16)
        for step in range(1, n_stn):
            prod_copy(lax.rem(p + step, n_stn), p, part).start()

    def place(ref, source, part):
        rows = slice(part * part_rows, (part + 1) * part_rows)
        to = pl.ds(source * chans + part * part_rows, part_rows)
        block = ref[rows]
        out_ref[to, 0] = block[:, :, :half]
        out_ref[to, 1] = block[:, :, half:]

    for part in range(n_part):
        place(prod.at[p], p, part)
        for step in range(1, n_stn):
            source = lax.rem(p + step, n_stn)
            prod_copy(source, source, part).wait_recv()
            place(gath.at[source], source, part)

    for step in range(1, n_chan):
        in_copy(lax.rem(q + step, n_chan), q).wait_send()

    def sent(step, carry):
        spec_copy(lax.rem(group + step, devices), me).wait_send()
        return carry

    lax.fori_loop(1, devices, sent, 0)
    for part in range(n_part):
        for step in range(1, n_stn):
            prod_copy(lax.rem(p + step, n_stn), p, part).wait_send()


def fused_device(n_stn, n_chan, voltages, filter_taps):
    inputs_here, frames_here, parts, points = voltages.shape
    devices = n_stn * n_chan
    frames = frames_here * n_chan
    inputs = inputs_here * n_stn
    each = inputs_here // n_chan
    chans = points // devices
    n_four, n_part = 8, 4
    split = voltages.reshape(n_chan, each, frames_here, parts, points)
    split = split.transpose(0, 1, 3, 2, 4).reshape(n_chan, each * parts, frames_here, points)
    matrix = jnp.asarray(fourier_rows(points))
    vmem = pl.BlockSpec(memory_space=pltpu.VMEM)
    return pl.pallas_call(
        functools.partial(fx_kernel, n_stn, n_chan, frames, points),
        out_shape=jax.ShapeDtypeStruct((points // n_chan, parts, inputs_here, inputs), jnp.bfloat16),
        in_specs=[vmem, vmem, pl.BlockSpec(memory_space=pl.ANY)],
        out_specs=vmem,
        scratch_shapes=[
            pltpu.VMEM((points, parts * points), jnp.bfloat16),
            pltpu.VMEM((n_chan, each * parts, frames_here, points), jnp.bfloat16),
            pltpu.VMEM((each * parts, points // LANES, frames + 16, LANES), jnp.float32),
            pltpu.VMEM((each * parts * frames, parts * points), jnp.bfloat16),
            pltpu.VMEM((points, LANES), jnp.bfloat16),
            pltpu.VMEM((devices, chans, LANES), jnp.bfloat16),
            pltpu.VMEM((inputs * chans, LANES), jnp.float32),
            pltpu.VMEM((n_stn, chans, inputs_here, LANES), jnp.bfloat16),
            pltpu.VMEM((n_stn, chans, inputs_here, LANES), jnp.bfloat16),
            pltpu.SemaphoreType.DMA((n_four,)),
            pltpu.SemaphoreType.DMA((n_chan,)),
            pltpu.SemaphoreType.DMA((n_chan,)),
            pltpu.SemaphoreType.DMA((devices,)),
            pltpu.SemaphoreType.DMA((devices,)),
            pltpu.SemaphoreType.DMA((n_part, n_stn)),
            pltpu.SemaphoreType.DMA((n_part, n_stn)),
        ],
        compiler_params=pltpu.CompilerParams(
            collective_id=0, has_side_effects=True, vmem_limit_bytes=48 * 1024 * 1024
        ),
    )(split, filter_taps, matrix)


def fits(n_stn, n_chan, voltages, filter_taps):
    inputs_here, frames_here, parts, points = voltages.shape
    devices = n_stn * n_chan
    return (
        inputs_here == SUB
        and frames_here == SUB
        and parts == 2
        and filter_taps.shape[0] <= 16
        and n_chan * 2 == inputs_here
        and 4 * n_chan * frames_here == LANES
        and inputs_here * n_stn * 2 == LANES
        and points % (devices * 32) == 0
    )


def on_device(n_stn, n_chan, voltages, filter_taps):
    if fits(n_stn, n_chan, voltages, filter_taps):
        return fused_device(n_stn, n_chan, voltages, filter_taps)
    return per_device(voltages, filter_taps)


def solution(mesh):
    placed = (P("stn", "chan", None, None), P())
    return jax.shard_map(
        functools.partial(on_device, mesh.shape["stn"], mesh.shape["chan"]),
        mesh=mesh,
        in_specs=placed,
        out_specs=P("chan", None, "stn", None),
        check_vma=False,
    )
```
